32 devices in a mesh: dp: 16 (over z, y, core), tensor: 2 (over x).
Axes of the slice: x: 2, y: 2, z: 4, core: 2. Of those that a mesh axis runs over, the one named last changes fastest.
Arguments:
- tokens: bfloat16 [6656, 1024], P('dp'), may hold values from -6 to 6
- cotangent: bfloat16 [6656, 1024], P('dp'), may hold values from -6 to 6
- norm1_gain: float32 [1024], replicated, may hold values from 0.5 to 1.5
- q_weight: bfloat16 [1024, 1024], P(None, 'tensor'), may hold values from -0.1875 to 0.1875
- k_weight: bfloat16 [1024, 512], P(None, 'tensor'), may hold values from -0.1875 to 0.1875
- v_weight: bfloat16 [1024, 512], P(None, 'tensor'), may hold values from -0.1875 to 0.1875
- q_gain: float32 [64], replicated, may hold values from 0.5 to 2.5
- k_gain: float32 [64], replicated, may hold values from 0.5 to 2.5
- o_weight: bfloat16 [1024, 1024], P('tensor'), may hold values from -0.75 to 0.75
- norm2_gain: float32 [1024], replicated, may hold values from 0.5 to 1.5
- gate_weight: bfloat16 [1024, 4608], P(None, 'tensor'), may hold values from -0.1875 to 0.1875
- up_weight: bfloat16 [1024, 4608], P(None, 'tensor'), may hold values from -0.1875 to 0.1875
- down_weight: bfloat16 [4608, 1024], P('tensor'), may hold values from -0.09375 to 0.09375
Outputs:
- output: bfloat16 [6656, 1024], P('dp')
- grad_tokens: float32 [6656, 1024], P('dp')
- grad_norm1_gain: float32 [1024], P('dp')
- grad_q_weight: float32 [1024, 1024], P('dp', 'tensor')
- grad_k_weight: float32 [1024, 512], P('dp', 'tensor')
- grad_v_weight: float32 [1024, 512], P('dp', 'tensor')
- grad_q_gain: float32 [64], P('dp')
- grad_k_gain: float32 [64], P('dp')
- grad_o_weight: float32 [1024, 1024], P('tensor', 'dp')
- grad_norm2_gain: float32 [1024], P('dp')
- grad_gate_weight: float32 [1024, 4608], P('dp', 'tensor')
- grad_up_weight: float32 [1024, 4608], P('dp', 'tensor')
- grad_down_weight: float32 [4608, 1024], P('tensor', 'dp')
The draws below stay inside these ranges and needn't reach their ends.
All inputs are finite; a program needn't handle non-finite values.
Results may differ from the reference program's by a relative error of at most 0.025.
Values sent between devices are 32-bit elements; how exact they have to be, the bound alone decides.
No kernel may reach another device: no remote copies, remote signals or barrier semaphores. Data moves between devices by JAX's collectives and lax.ppermute only.
A program may use at most 192 MiB of HBM per device.

```python
import math
import jax
import jax.numpy as jnp
from jax import lax

D = 1024
HQ = 16
KV = 8
HD = 64
FF = 4608
L = 416
SEQS = 16
TOKENS = 6656


def shard_levels(own_key, shape, cuts, least, largest):
    def one(dim, shards_of):
        heights = jax.random.uniform(jax.random.fold_in(jax.random.fold_in(own_key, 6), dim), (shards_of,), jnp.float32, least / len(cuts), largest / len(cuts))
        return jnp.repeat(jnp.exp(heights), shape[dim] // shards_of).reshape((-1,) + (1,) * (len(shape) - dim - 1))

    level = one(*cuts[0])
    for cut in cuts[1:]:
        level = level * one(*cut)
    return level


def centred(rng, shape, scale, most, split=(), kind=jnp.bfloat16):
    factor_of = shard_levels(rng, shape, split, -0.22, 0.18) if split else 1.0
    drawn = jax.random.normal(rng, shape, jnp.float32) * scale * factor_of
    return jnp.minimum(jnp.maximum(drawn, -most), most).astype(kind)


def setup_inputs(seed: int = 0) -> dict:
    arg_keys = jax.random.split(jax.random.key(seed), 14)
    tokens = centred(arg_keys[0], (TOKENS, D), 1.0, 6.0, ((0, 16),))
    cotangent = centred(arg_keys[1], (TOKENS, D), 1.0, 6.0, ((0, 16),))
    norm1_gain = jnp.clip(1.0 + 0.1 * jax.random.normal(arg_keys[2], (D,), jnp.float32), 0.5, 1.5)
    q_weight = centred(arg_keys[3], (D, HQ * HD), D ** -0.5, 0.1875, ((1, 2),))
    k_weight = centred(arg_keys[4], (D, KV * HD), D ** -0.5, 0.1875, ((1, 2),))
    v_weight = centred(arg_keys[5], (D, KV * HD), D ** -0.5, 0.1875, ((1, 2),))
    q_gain = jnp.clip(jnp.exp(jax.random.uniform(arg_keys[6], (HD,), jnp.float32, math.log(0.5), math.log(2.5))), 0.5, 2.5)
    k_gain = jnp.clip(jnp.exp(jax.random.uniform(arg_keys[7], (HD,), jnp.float32, math.log(0.5), math.log(2.5))), 0.5, 2.5)
    o_weight = centred(arg_keys[8], (HQ * HD, D), (HQ * HD // 16) ** -0.5, 0.75, ((0, 2),))
    norm2_gain = jnp.clip(1.0 + 0.1 * jax.random.normal(arg_keys[9], (D,), jnp.float32), 0.5, 1.5)
    gate_weight = centred(arg_keys[10], (D, FF), D ** -0.5, 0.1875, ((1, 2),))
    up_weight = centred(arg_keys[11], (D, FF), D ** -0.5, 0.1875, ((1, 2),))
    down_weight = centred(arg_keys[12], (FF, D), FF ** -0.5, 0.09375, ((0, 2),))
    return {"tokens": tokens, "cotangent": cotangent, "norm1_gain": norm1_gain, "q_weight": q_weight, "k_weight": k_weight, "v_weight": v_weight, "q_gain": q_gain, "k_gain": k_gain, "o_weight": o_weight, "norm2_gain": norm2_gain, "gate_weight": gate_weight, "up_weight": up_weight, "down_weight": down_weight}


EPS = 1e-06
THETA = 1000000.0

def rotate(value):
    half = value.shape[-1] // 2
    return jnp.concatenate([-value[..., half:], value[..., :half]], axis=-1)

def tables(length, width):
    half = width // 2
    freq = THETA ** (-(jnp.arange(half, dtype=jnp.float32) * 2.0 / width))
    angle = jnp.arange(length, dtype=jnp.float32)[:, None] * freq[None, :]
    cosine = jnp.concatenate([jnp.cos(angle), jnp.cos(angle)], axis=1)
    sine = jnp.concatenate([jnp.sin(angle), jnp.sin(angle)], axis=1)
    return (cosine, sine)

def rms_forward(value, gain):
    factor = lax.rsqrt(lax.optimization_barrier(jnp.mean(value * value, axis=-1, keepdims=True)) + EPS)
    normed = value * factor
    return (normed * gain, normed, factor)

def rms_backward(grad_out, normed, factor, gain):
    grad_hat = grad_out * gain
    grad_in = factor * (grad_hat - normed * lax.optimization_barrier(jnp.mean(grad_hat * normed, axis=-1, keepdims=True)))
    return (grad_in, grad_out * normed)

def f32(value):
    return value.astype(jnp.float32)

def reference(tokens, cotangent, norm1_gain, q_weight, k_weight, v_weight, q_gain, k_gain, o_weight, norm2_gain, gate_weight, up_weight, down_weight):
    group = HQ // KV
    scaling = HD ** (-0.5)
    cosine, sine = tables(L, HD)
    cosine = cosine[:, None, :]
    sine = sine[:, None, :]
    place = jnp.arange(L)
    causal = place[:, None] >= place[None, :]
    token_seqs = tokens.reshape(SEQS, L, D)
    grad_seqs = cotangent.reshape(SEQS, L, D)

    def one_sequence(carry, pair):
        seq_in, seq_grad = pair
        inputs = f32(seq_in)
        normed1, hat1, factor1 = rms_forward(inputs, norm1_gain)
        n1 = normed1.astype(jnp.bfloat16)
        queries = jnp.dot(n1, q_weight, preferred_element_type=jnp.float32).reshape(L, HQ, HD)
        keys = jnp.dot(n1, k_weight, preferred_element_type=jnp.float32).reshape(L, KV, HD)
        values = jnp.dot(n1, v_weight, preferred_element_type=jnp.float32).astype(jnp.bfloat16).reshape(L, KV, HD)
        q_normed, q_hat, q_factor = rms_forward(queries, q_gain)
        k_normed, k_hat, k_factor = rms_forward(keys, k_gain)
        q_rot = (q_normed * cosine + rotate(q_normed) * sine).astype(jnp.bfloat16)
        k_rot = (k_normed * cosine + rotate(k_normed) * sine).astype(jnp.bfloat16)
        keys_all = jnp.repeat(k_rot, group, axis=1)
        vals_all = jnp.repeat(values, group, axis=1)
        scores = jnp.einsum('qhd,khd->hqk', f32(q_rot), f32(keys_all)) * scaling
        scores = jnp.where(causal[None], scores, -1e+30)
        peak = lax.optimization_barrier(jnp.max(scores, axis=-1, keepdims=True))
        lse = peak + jnp.log(lax.optimization_barrier(jnp.sum(jnp.exp(scores - peak), axis=-1, keepdims=True)))
        prob = jnp.exp(scores - lse)
        prob_b = prob.astype(jnp.bfloat16)
        attended = jnp.einsum('hqk,khd->qhd', f32(prob_b), f32(vals_all)).astype(jnp.bfloat16).reshape(L, HQ * HD)
        hidden = inputs + jnp.dot(attended, o_weight, preferred_element_type=jnp.float32)
        normed2, hat2, factor2 = rms_forward(hidden, norm2_gain)
        n2 = normed2.astype(jnp.bfloat16)
        gate = jnp.dot(n2, gate_weight, preferred_element_type=jnp.float32)
        up = jnp.dot(n2, up_weight, preferred_element_type=jnp.float32)
        sig = jax.nn.sigmoid(gate)
        silu_gate = gate * sig
        inner = (silu_gate * up).astype(jnp.bfloat16)
        result = hidden + jnp.dot(inner, down_weight, preferred_element_type=jnp.float32)
        output = result.astype(jnp.bfloat16)
        grad_down = jnp.dot(inner.T, seq_grad, preferred_element_type=jnp.float32)
        grad_inner = jnp.dot(seq_grad, down_weight.T, preferred_element_type=jnp.float32)
        grad_gate = (grad_inner * up * (sig * (1.0 + gate * (1.0 - sig)))).astype(jnp.bfloat16)
        grad_up = (grad_inner * silu_gate).astype(jnp.bfloat16)
        grad_gate_w = jnp.dot(n2.T, grad_gate, preferred_element_type=jnp.float32)
        grad_up_w = jnp.dot(n2.T, grad_up, preferred_element_type=jnp.float32)
        grad_n2 = jnp.dot(grad_gate, gate_weight.T, preferred_element_type=jnp.float32) + jnp.dot(grad_up, up_weight.T, preferred_element_type=jnp.float32)
        grad_hidden_n, gain2_rows = rms_backward(grad_n2, hat2, factor2, norm2_gain)
        grad_hidden = f32(seq_grad) + grad_hidden_n
        grad_hidden_b = grad_hidden.astype(jnp.bfloat16)
        grad_o = jnp.dot(attended.T, grad_hidden_b, preferred_element_type=jnp.float32)
        grad_att = jnp.dot(grad_hidden_b, o_weight.T, preferred_element_type=jnp.float32).astype(jnp.bfloat16).reshape(L, HQ, HD)
        dprob = jnp.einsum('qhd,khd->hqk', f32(grad_att), f32(vals_all))
        dscore = prob * (dprob - lax.optimization_barrier(jnp.sum(prob * dprob, axis=-1, keepdims=True)))
        dscore_b = (dscore * scaling).astype(jnp.bfloat16)
        grad_vals = jnp.einsum('hqk,qhd->khd', f32(prob_b), f32(grad_att)).reshape(L, KV, group, HD).sum(axis=2)
        grad_qrot = jnp.einsum('hqk,khd->qhd', f32(dscore_b), f32(keys_all))
        grad_krot = jnp.einsum('hqk,qhd->khd', f32(dscore_b), f32(q_rot)).reshape(L, KV, group, HD).sum(axis=2)
        grad_qn = grad_qrot * cosine - rotate(grad_qrot * sine)
        grad_kn = grad_krot * cosine - rotate(grad_krot * sine)
        grad_q, q_rows = rms_backward(grad_qn, q_hat, q_factor, q_gain)
        grad_k, k_rows = rms_backward(grad_kn, k_hat, k_factor, k_gain)
        grad_q_b = grad_q.astype(jnp.bfloat16).reshape(L, HQ * HD)
        grad_k_b = grad_k.astype(jnp.bfloat16).reshape(L, KV * HD)
        grad_v_b = grad_vals.astype(jnp.bfloat16).reshape(L, KV * HD)
        grad_q_w = jnp.dot(n1.T, grad_q_b, preferred_element_type=jnp.float32)
        grad_k_w = jnp.dot(n1.T, grad_k_b, preferred_element_type=jnp.float32)
        grad_v_w = jnp.dot(n1.T, grad_v_b, preferred_element_type=jnp.float32)
        grad_n1 = jnp.dot(grad_q_b, q_weight.T, preferred_element_type=jnp.float32) + jnp.dot(grad_k_b, k_weight.T, preferred_element_type=jnp.float32) + jnp.dot(grad_v_b, v_weight.T, preferred_element_type=jnp.float32)
        grad_in_n, gain1_rows = rms_backward(grad_n1, hat1, factor1, norm1_gain)
        grad_in = grad_hidden + grad_in_n
        terms = (lax.optimization_barrier(jnp.sum(gain1_rows, axis=0)), grad_q_w, grad_k_w, grad_v_w, lax.optimization_barrier(jnp.sum(q_rows, axis=(0, 1))), lax.optimization_barrier(jnp.sum(k_rows, axis=(0, 1))), grad_o, lax.optimization_barrier(jnp.sum(gain2_rows, axis=0)), grad_gate_w, grad_up_w, grad_down)
        carry = tuple((total + term for total, term in zip(carry, terms)))
        return (carry, (output, grad_in))
    zeros = (jnp.zeros((D,), jnp.float32), jnp.zeros((D, HQ * HD), jnp.float32), jnp.zeros((D, KV * HD), jnp.float32), jnp.zeros((D, KV * HD), jnp.float32), jnp.zeros((HD,), jnp.float32), jnp.zeros((HD,), jnp.float32), jnp.zeros((HQ * HD, D), jnp.float32), jnp.zeros((D,), jnp.float32), jnp.zeros((D, FF), jnp.float32), jnp.zeros((D, FF), jnp.float32), jnp.zeros((FF, D), jnp.float32))
    totals, stacked = lax.scan(one_sequence, zeros, (token_seqs, grad_seqs))
    output = stacked[0].reshape(TOKENS, D)
    grad_tokens = stacked[1].reshape(TOKENS, D)
    return (output, grad_tokens, totals[0], totals[1], totals[2], totals[3], totals[4], totals[5], totals[6], totals[7], totals[8], totals[9], totals[10])
```

```python
import jax
import jax.numpy as jnp
from jax import lax
from jax.experimental import pallas as pl
from jax.experimental.pallas import tpu as pltpu
from jax.sharding import PartitionSpec as P

HD = 64
L = 416
EPS = 1e-06
THETA = 1000000.0
LANES = 2 * HD


def rope_tables(length):
    half = HD // 2
    freq = THETA ** (-(jnp.arange(half, dtype=jnp.float32) * 2.0 / HD))
    angle = jnp.arange(length, dtype=jnp.float32)[:, None] * freq[None, :]
    return jnp.tile(jnp.cos(angle), (1, 4)), jnp.tile(jnp.sin(angle), (1, 4))


def lane_of(shape):
    return lax.broadcasted_iota(jnp.int32, shape, 1)


def first_head(shape):
    return lane_of(shape) < HD


def half_mean(value):
    first = first_head(value.shape)
    low = jnp.sum(jnp.where(first, value, 0.0), axis=1, keepdims=True)
    high = jnp.sum(jnp.where(first, 0.0, value), axis=1, keepdims=True)
    return jnp.where(first, low, high) * (1.0 / HD)


def rotate_pair(value):
    turned = pltpu.roll(value, HD // 2, 1)
    ahead = pltpu.roll(value, LANES - HD // 2, 1)
    return jnp.where(lane_of(value.shape) % HD < HD // 2, -ahead, turned)


def head_norm(value, gain):
    factor = lax.rsqrt(half_mean(value * value) + EPS)
    hat = value * factor
    return hat * gain, hat, factor


def rope_pair(value, cosine, sine):
    return (value * cosine + rotate_pair(value) * sine).astype(jnp.bfloat16)


def head_norm_backward(grad_rot, hat, factor, gain, cosine, sine):
    grad_out = grad_rot * cosine - rotate_pair(grad_rot * sine)
    grad_hat = grad_out * gain
    grad_in = factor * (grad_hat - hat * half_mean(grad_hat * hat))
    return grad_in, jnp.sum(grad_out * hat, axis=0, keepdims=True)


def widen(value):
    return value if value.shape[1] == LANES else jnp.concatenate([value, value], axis=1)


def both_halves(value, which):
    swapped = pltpu.roll(value.astype(jnp.float32), HD, 1).astype(value.dtype)
    first = first_head(value.shape)
    return jnp.where(first, value, swapped) if which == 0 else jnp.where(first, swapped, value)


def fold(value):
    return value + pltpu.roll(value, HD, 1)


def only(value, head):
    first = first_head(value.shape)
    zero = jnp.zeros_like(value)
    return jnp.where(first, value, zero) if head == 0 else jnp.where(first, zero, value)


def product(left, right, dims):
    return lax.dot_general(left, right, (dims, ((), ())), preferred_element_type=jnp.float32)


def causal_scores(query, key):
    scores = product(query, key, ((1,), (1,))) * (HD ** -0.5)
    rows = lax.broadcasted_iota(jnp.int32, scores.shape, 0)
    cols = lax.broadcasted_iota(jnp.int32, scores.shape, 1)
    return jnp.where(rows >= cols, scores, -1e30)


def forward_kernel(q_ref, k_ref, v_ref, qg_ref, kg_ref, cos_ref, sin_ref, att_ref, wide_ref, lse_ref):
    cosine, sine = cos_ref[...], sin_ref[...]
    groups = q_ref.shape[1] // LANES
    k_rot = rope_pair(head_norm(widen(k_ref[...]), kg_ref[...])[0], cosine, sine)
    vals = widen(v_ref[...])
    for g in range(groups):
        span = slice(g * LANES, (g + 1) * LANES)
        q_rot = rope_pair(head_norm(q_ref[:, span], qg_ref[...])[0], cosine, sine)
        key, val = both_halves(k_rot, g), both_halves(vals, g)
        att, lse = [], []
        for head in range(2):
            scores = causal_scores(only(q_rot, head), key)
            peak = jnp.max(scores, axis=1, keepdims=True)
            expo = jnp.exp(scores - peak)
            total = jnp.sum(expo, axis=1, keepdims=True)
            lse.append(peak + jnp.log(total))
            prob = (expo * (1.0 / total)).astype(jnp.bfloat16)
            att.append(product(prob, val, ((1,), (0,))))
        first = first_head(att[0].shape)
        rounded = jnp.where(first, att[0], att[1]).astype(jnp.bfloat16)
        att_ref[:, span] = rounded
        wide_ref[:, span] = rounded.astype(jnp.float32)
        lse_ref[:, span] = jnp.where(first, lse[0], lse[1])


def backward_kernel(
    q_ref, k_ref, v_ref, qg_ref, kg_ref, cos_ref, sin_ref, lse_ref, ga_ref,
    gq_ref, gk_ref, gv_ref, gains_ref,
):
    cosine, sine = cos_ref[...], sin_ref[...]
    groups = q_ref.shape[1] // LANES
    k_normed, k_hat, k_factor = head_norm(widen(k_ref[...]), kg_ref[...])
    k_rot = rope_pair(k_normed, cosine, sine)
    vals = widen(v_ref[...])
    grad_k, grad_v = [], []
    q_gain = jnp.zeros((1, LANES), jnp.float32)
    for g in range(groups):
        span = slice(g * LANES, (g + 1) * LANES)
        q_normed, q_hat, q_factor = head_norm(q_ref[:, span], qg_ref[...])
        q_rot = rope_pair(q_normed, cosine, sine)
        key, val = both_halves(k_rot, g), both_halves(vals, g)
        grad_q_heads = []
        grad_key = grad_val = None
        for head in range(2):
            query = only(q_rot, head)
            grad_att = only(ga_ref[:, span], head)
            lse = lse_ref[:, g * LANES + head * HD : g * LANES + head * HD + 1]
            prob = jnp.exp(causal_scores(query, key) - lse)
            dprob = product(grad_att, val, ((1,), (1,)))
            inner = jnp.sum(prob * dprob, axis=1, keepdims=True)
            dscore = (prob * (dprob - inner) * (HD ** -0.5)).astype(jnp.bfloat16)
            grad_q_heads.append(product(dscore, key, ((1,), (0,))))
            to_key = product(dscore, query, ((0,), (0,)))
            to_val = product(prob.astype(jnp.bfloat16), grad_att, ((0,), (0,)))
            grad_key = to_key if grad_key is None else grad_key + to_key
            grad_val = to_val if grad_val is None else grad_val + to_val
        first = first_head(q_hat.shape)
        grad_rot = jnp.where(first, grad_q_heads[0], grad_q_heads[1])
        grad_q, rows = head_norm_backward(grad_rot, q_hat, q_factor, qg_ref[...], cosine, sine)
        gq_ref[:, span] = grad_q.astype(jnp.bfloat16)
        q_gain = q_gain + rows
        grad_k.append(fold(grad_key))
        grad_v.append(fold(grad_val))
    first = first_head(k_hat.shape)
    grad_rot = grad_k[0] if groups == 1 else jnp.where(first, grad_k[0], grad_k[1])
    grad_val = grad_v[0] if groups == 1 else jnp.where(first, grad_v[0], grad_v[1])
    grad_key, k_gain = head_norm_backward(grad_rot, k_hat, k_factor, kg_ref[...], cosine, sine)
    if k_ref.shape[1] != LANES:
        grad_key, grad_val = grad_key[:, :HD], grad_val[:, :HD]
        k_gain = jnp.where(first_head(k_gain.shape), k_gain, 0.0)
    gk_ref[...] = grad_key.astype(jnp.bfloat16)
    gv_ref[...] = grad_val.astype(jnp.bfloat16)
    row = lax.broadcasted_iota(jnp.int32, (8, LANES), 0)
    gains_ref[...] = jnp.where(row == 0, q_gain, jnp.where(row == 1, k_gain, 0.0))


def attention_specs(q_cols, k_cols):
    groups = min(2, k_cols // HD)
    q_spec = pl.BlockSpec((L, groups * LANES), lambda s, i: (s, i))
    k_spec = pl.BlockSpec((L, groups * HD), lambda s, i: (s, i))
    one = pl.BlockSpec((1, LANES), lambda s, i: (0, 0))
    table = pl.BlockSpec((L, LANES), lambda s, i: (0, 0))
    return q_cols // (groups * LANES), q_spec, k_spec, one, table


def attention_forward(queries, keys, values, q_gain, k_gain, cosine, sine):
    rows, q_cols = queries.shape
    steps, q_spec, k_spec, one, table = attention_specs(q_cols, keys.shape[1])
    return pl.pallas_call(
        forward_kernel,
        grid=(rows // L, steps),
        in_specs=[q_spec, k_spec, k_spec, one, one, table, table],
        out_specs=[q_spec, q_spec, q_spec],
        out_shape=[
            jax.ShapeDtypeStruct((rows, q_cols), jnp.bfloat16),
            jax.ShapeDtypeStruct((rows, q_cols), jnp.float32),
            jax.ShapeDtypeStruct((rows, q_cols), jnp.float32),
        ],
        compiler_params=pltpu.CompilerParams(vmem_limit_bytes=48 << 20),
        name="attention_forward",
    )(queries, keys, values, q_gain, k_gain, cosine, sine)


def attention_backward(queries, keys, values, q_gain, k_gain, cosine, sine, lse, grad_att):
    rows, q_cols = queries.shape
    k_cols = keys.shape[1]
    steps, q_spec, k_spec, one, table = attention_specs(q_cols, k_cols)
    seqs = rows // L
    return pl.pallas_call(
        backward_kernel,
        grid=(seqs, steps),
        in_specs=[q_spec, k_spec, k_spec, one, one, table, table, q_spec, q_spec],
        out_specs=[q_spec, k_spec, k_spec, pl.BlockSpec((8, LANES), lambda s, i: (s * steps + i, 0))],
        out_shape=[
            jax.ShapeDtypeStruct((rows, q_cols), jnp.bfloat16),
            jax.ShapeDtypeStruct((rows, k_cols), jnp.bfloat16),
            jax.ShapeDtypeStruct((rows, k_cols), jnp.bfloat16),
            jax.ShapeDtypeStruct((seqs * steps * 8, LANES), jnp.float32),
        ],
        compiler_params=pltpu.CompilerParams(vmem_limit_bytes=48 << 20),
        name="attention_backward",
    )(queries, keys, values, q_gain, k_gain, cosine, sine, lse, grad_att)


def rms_forward(value, gain):
    factor = lax.rsqrt(jnp.mean(value * value, axis=-1, keepdims=True) + EPS)
    normed = value * factor
    return (normed * gain, normed, factor)


def rms_backward(grad_out, normed, factor, gain):
    grad_hat = grad_out * gain
    grad_in = factor * (grad_hat - normed * jnp.mean(grad_hat * normed, axis=-1, keepdims=True))
    return (grad_in, grad_out * normed)


def matmul(left, right):
    return jnp.dot(left, right, preferred_element_type=jnp.float32)


def against(left, right):
    return lax.dot_general(
        left, right, (((1,), (1,)), ((), ())), preferred_element_type=jnp.float32
    )


def tensor_sum(value):
    if lax.axis_size("tensor") != 2:
        return lax.psum(value, "tensor")
    return value + lax.ppermute(value, "tensor", [(0, 1), (1, 0)])


def flip_pairs(bit):
    return [(i, i ^ bit) for i in range(lax.axis_size("dp"))]


def line_order(line, place):
    if line == 4:
        return lambda pos: jnp.where(place < 2, 3 - pos, pos)
    return lambda pos: (place + pos) % line


def row_picker(model, line_first):
    size = lax.axis_size("dp")
    me = lax.axis_index("dp")
    line, block = size // 4, model // size
    spot = jnp.arange(model)
    inside = spot % block
    core = 1 - spot // (model // 2)
    unit = (spot // block) % (2 * line)
    if line_first:
        pos, near = unit // 2, 1 - unit % 2
    else:
        pos, near = unit % line, 1 - unit // line
    place = line_order(line, me // 4)(pos)
    device = place * 4 + ((me % 4) ^ (core + 2 * near))
    rows = device * block + inside
    return (rows[:, None] == jnp.arange(model)[None, :]).astype(jnp.bfloat16)


def pick_rows(pick, value):
    return against(pick, value).astype(jnp.bfloat16)


def line_scatter(value):
    size = lax.axis_size("dp")
    place = lax.axis_index("dp") // 4
    line = size // 4
    block = value.shape[0] // line
    if line == 4:
        span = lambda array, start, stop: array[start * block : stop * block]
        ends = [(i, i + 4) for i in range(4)] + [(i + 12, i + 8) for i in range(4)]
        middle = [(i + 4, i + 8) for i in range(4)] + [(i + 8, i + 4) for i in range(4)]
        back = [(i + 4, i) for i in range(4)] + [(i + 8, i + 12) for i in range(4)]
        first = lax.ppermute(span(value, 0, 3), "dp", ends)
        second = lax.ppermute(span(value, 0, 2) + span(first, 0, 2), "dp", middle)
        third = lax.ppermute(span(value, 3, 4) + span(second, 0, 1), "dp", back)
        at_end = (place == 0) | (place == 3)
        own = jnp.where(at_end, span(value, 3, 4), span(value, 2, 3))
        return own + span(first, 2, 3) + span(second, 1, 2) + third
    part = lambda pos: value[pos * block : (pos + 1) * block]
    up = down = None
    for step in range(1, line):
        to_up = part(line - step) if up is None else part(line - step) + up
        to_down = part(step) if down is None else part(step) + down
        up = lax.ppermute(to_up, "dp", [(i, i + 4) for i in range(4 * step)])
        down = lax.ppermute(to_down, "dp", [(i, i - 4) for i in range(size - 4 * step, size)])
    return part(0) if up is None else part(0) + up + down


def scatter_near_first(rows, value):
    half, quarter = rows.shape[0] // 2, rows.shape[0] // 4
    got = lax.ppermute(matmul(rows[:half], value), "dp", flip_pairs(1))
    far = matmul(rows[half : half + quarter], value) + got[:quarter]
    from_far = lax.ppermute(far, "dp", flip_pairs(2))
    return line_scatter(matmul(rows[half + quarter :], value) + got[quarter:] + from_far)


def scatter_line_first(rows, value):
    half = rows.shape[0] // 2
    got = lax.ppermute(matmul(rows[:half], value), "dp", flip_pairs(1))
    both = line_scatter(matmul(rows[half:], value) + got)
    block = both.shape[0] // 2
    return both[block:] + lax.ppermute(both[:block], "dp", flip_pairs(2))


def scatter_small(value):
    value = tensor_sum(value)
    size = lax.axis_size("dp")
    me = lax.axis_index("dp")
    line = size // 4
    places = line_order(line, me // 4)(jnp.arange(line))
    take = lambda flip: value[places * 4 + ((me % 4) ^ flip)]
    got = lax.ppermute(jnp.concatenate([take(3), take(1)]), "dp", flip_pairs(1))
    far = lax.ppermute(take(2) + got[:line], "dp", flip_pairs(2))
    return line_scatter(take(0) + got[line:] + far)


def other_weight(weight):
    part = lax.axis_index("dp") % 4
    quarter = weight.shape[0] // 4
    mine = lax.dynamic_slice_in_dim(weight, part * quarter, quarter).astype(jnp.float32)
    got = lax.ppermute(mine, "tensor", [(0, 1), (1, 0)])
    near = jnp.stack([got, lax.ppermute(got, "dp", flip_pairs(2))])
    both = jnp.stack([near, lax.ppermute(near, "dp", flip_pairs(1))])
    both = jnp.where(part % 2 == 1, both[::-1], both)
    both = jnp.where(part // 2 == 1, both[:, ::-1], both)
    return jnp.swapaxes(both, 0, 1).reshape(weight.shape)


def join_kernel(
    side_ref, tok_ref, own_ref, got_ref, own_w_ref, got_w_ref, gain_ref,
    hidden_ref, n2_ref, hat_ref, factor_ref,
):
    own = product(own_ref[...], own_w_ref[...], ((1,), (0,)))
    got = product(
        got_ref[...].astype(jnp.bfloat16), got_w_ref[...].astype(jnp.bfloat16), ((1,), (0,))
    )
    low_first = side_ref[0] == 0
    hidden = tok_ref[...].astype(jnp.float32) + jnp.where(low_first, own + got, got + own)
    factor = lax.rsqrt(jnp.mean(hidden * hidden, axis=1, keepdims=True) + EPS)
    hat = hidden * factor
    hidden_ref[...] = hidden
    hat_ref[...] = hat
    factor_ref[...] = factor
    n2_ref[...] = (hat * gain_ref[...]).astype(jnp.bfloat16)


def join_heads(side, tokens, own, got, own_weight, got_weight, gain):
    rows, model = tokens.shape
    units = own.shape[1]
    whole = lambda height, width: pl.BlockSpec((height, width), lambda i, side: (0, 0))
    part = rows // 2 if rows % 32 == 0 else rows
    split = lambda width: pl.BlockSpec((part, width), lambda i, side: (i, 0))
    return pl.pallas_call(
        join_kernel,
        grid_spec=pltpu.PrefetchScalarGridSpec(
            num_scalar_prefetch=1,
            grid=(rows // part,),
            in_specs=[
                split(model), split(units), split(units),
                whole(units, model), whole(units, model), whole(1, model),
            ],
            out_specs=[split(model), split(model), split(model), split(1)],
        ),
        out_shape=[
            jax.ShapeDtypeStruct((rows, model), jnp.float32),
            jax.ShapeDtypeStruct((rows, model), jnp.bfloat16),
            jax.ShapeDtypeStruct((rows, model), jnp.float32),
            jax.ShapeDtypeStruct((rows, 1), jnp.float32),
        ],
        compiler_params=pltpu.CompilerParams(vmem_limit_bytes=48 << 20),
        name="join_heads",
    )(side[None], tokens, own, got, own_weight, got_weight, gain[None])


def on_device(
    tokens,
    cotangent,
    norm1_gain,
    q_weight,
    k_weight,
    v_weight,
    q_gain,
    k_gain,
    o_weight,
    norm2_gain,
    gate_weight,
    up_weight,
    down_weight,
):
    model = tokens.shape[1]
    size = lax.axis_size("dp")
    pair = lax.axis_size("tensor") == 2
    side = lax.axis_index("tensor")
    cosine, sine = rope_tables(L)
    q_gain2 = jnp.tile(q_gain, 2)[None]
    k_gain2 = jnp.tile(k_gain, 2)[None]
    if pair:
        o_other = other_weight(o_weight)
    inputs = tokens.astype(jnp.float32)
    normed1, hat1, factor1 = rms_forward(inputs, norm1_gain)
    n1 = normed1.astype(jnp.bfloat16)
    queries = matmul(n1, q_weight)
    keys = matmul(n1, k_weight)
    values = matmul(n1, v_weight).astype(jnp.bfloat16)
    attended, att_wide, lse = attention_forward(
        queries, keys, values, q_gain2, k_gain2, cosine, sine
    )
    near_pick = row_picker(model, False)
    line_pick = row_picker(model, True)
    cot_line = pick_rows(line_pick, cotangent)
    cot_near = pick_rows(near_pick, cotangent)
    grad_inner = against(cotangent, down_weight)
    if pair:
        att_got = lax.ppermute(att_wide, "tensor", [(0, 1), (1, 0)])
        hidden, n2, hat2, factor2 = join_heads(
            side, tokens, attended, att_got, o_weight, o_other, norm2_gain
        )
    else:
        hidden = inputs + tensor_sum(matmul(attended, o_weight))
        normed2, hat2, factor2 = rms_forward(hidden, norm2_gain)
        n2 = normed2.astype(jnp.bfloat16)
    n2_near = pick_rows(near_pick, n2)
    width = gate_weight.shape[1]
    cut = width // 3
    downs, gates, ups = [], [], []
    out_part = grad_n2_part = None
    for piece in range(3):
        span = slice(piece * cut, (piece + 1) * cut)
        gate = matmul(n2, gate_weight[:, span])
        up = matmul(n2, up_weight[:, span])
        sig = jax.nn.sigmoid(gate)
        silu_gate = gate * sig
        inner = (silu_gate * up).astype(jnp.bfloat16)
        grad_in = grad_inner[:, span]
        grad_gate = (grad_in * up * (sig * (1.0 + gate * (1.0 - sig)))).astype(jnp.bfloat16)
        grad_up = (grad_in * silu_gate).astype(jnp.bfloat16)
        if piece < 2:
            downs.append(scatter_line_first(cot_line, inner))
        else:
            downs.append(scatter_near_first(cot_near, inner))
        both = scatter_near_first(n2_near, jnp.concatenate([grad_gate, grad_up], axis=1))
        gates.append(both[:, :cut])
        ups.append(both[:, cut:])
        out = matmul(inner, down_weight[span])
        back = against(grad_gate, gate_weight[:, span]) + against(grad_up, up_weight[:, span])
        out_part = out if out_part is None else out_part + out
        grad_n2_part = back if grad_n2_part is None else grad_n2_part + back
    sum_down_t = jnp.concatenate(downs, axis=1)
    sum_gate_w = jnp.concatenate(gates, axis=1)
    sum_up_w = jnp.concatenate(ups, axis=1)
    grad_gain2 = jnp.sum(grad_n2_part * hat2, axis=0)
    grad_n2 = tensor_sum(grad_n2_part)
    result = hidden + tensor_sum(out_part)
    output = result.astype(jnp.bfloat16)
    grad_hidden_n, _ = rms_backward(grad_n2, hat2, factor2, norm2_gain)
    grad_hidden = cotangent.astype(jnp.float32) + grad_hidden_n
    grad_hidden_b = grad_hidden.astype(jnp.bfloat16)
    hidden_near = pick_rows(near_pick, grad_hidden_b)
    sum_o_t = scatter_near_first(hidden_near, attended)
    grad_att = against(grad_hidden_b, o_weight).astype(jnp.bfloat16)
    grad_q_b, grad_k_b, grad_v_b, head_gains = attention_backward(
        queries, keys, values, q_gain2, k_gain2, cosine, sine, lse, grad_att
    )
    head_gains = jnp.sum(head_gains.reshape(-1, 8, 2, HD), axis=(0, 2))
    grad_n1_part = (
        against(grad_q_b, q_weight) + against(grad_k_b, k_weight) + against(grad_v_b, v_weight)
    )
    grad_gain1 = jnp.sum(grad_n1_part * hat1, axis=0)
    grad_n1 = tensor_sum(grad_n1_part)
    grad_in_n, _ = rms_backward(grad_n1, hat1, factor1, norm1_gain)
    grad_tokens = grad_hidden + grad_in_n
    n1_near = pick_rows(near_pick, n1)
    sum_qkv = scatter_near_first(n1_near, jnp.concatenate([grad_q_b, grad_k_b, grad_v_b], axis=1))
    q_cols, k_cols = grad_q_b.shape[1], grad_k_b.shape[1]
    gains = jnp.concatenate(
        [
            grad_gain1.reshape(size, -1),
            grad_gain2.reshape(size, -1),
            head_gains[0].reshape(size, -1),
            head_gains[1].reshape(size, -1),
        ],
        axis=1,
    )
    sum_gains = scatter_small(gains)[0]
    wide, narrow = model // size, HD // size
    return (
        output,
        grad_tokens,
        sum_gains[:wide],
        sum_qkv[:, :q_cols],
        sum_qkv[:, q_cols : q_cols + k_cols],
        sum_qkv[:, q_cols + k_cols :],
        sum_gains[2 * wide : 2 * wide + narrow],
        sum_gains[2 * wide + narrow :],
        sum_o_t.T,
        sum_gains[wide : 2 * wide],
        sum_gate_w,
        sum_up_w,
        sum_down_t.T,
    )


def solution(mesh):
    placed = (
        P("dp", None),
        P("dp", None),
        P(),
        P(None, "tensor"),
        P(None, "tensor"),
        P(None, "tensor"),
        P(),
        P(),
        P("tensor", None),
        P(),
        P(None, "tensor"),
        P(None, "tensor"),
        P("tensor", None),
    )
    return jax.shard_map(
        on_device,
        mesh=mesh,
        in_specs=placed,
        out_specs=(
            P("dp", None),
            P("dp", None),
            P("dp"),
            P("dp", "tensor"),
            P("dp", "tensor"),
            P("dp", "tensor"),
            P("dp"),
            P("dp"),
            P("tensor", "dp"),
            P("dp"),
            P("dp", "tensor"),
            P("dp", "tensor"),
            P("tensor", "dp"),
        ),
        check_vma=False,
    )
```
